32 devices in a mesh: dp: 4 (over y, core), seq: 8 (over z, x).
Axes of the slice: x: 2, y: 2, z: 4, core: 2. Of those that a mesh axis runs over, the one named last changes fastest.
Arguments:
- tokens: bfloat16 [2, 8, 1024, 768], P(None, 'dp', 'seq'), may hold values from -6 to 6
- doc_starts: int32 [2, 8, 4], P(None, 'dp'), may hold values from 0 to 1023, as said below
- cotangent: bfloat16 [2, 8, 1024, 768], P(None, 'dp', 'seq'), may hold values from -6 to 6
- norm1_gain: bfloat16 [768], P(('dp', 'seq')), may hold values from 0.099609375 to 1.8984375
- norm1_shift: bfloat16 [768], P(('dp', 'seq')), may hold values from -3 to 3
- query_weight: bfloat16 [768, 768], P(('dp', 'seq')), may hold values from -0.21875 to 0.21875
- query_bias: bfloat16 [768], P(('dp', 'seq')), may hold values from -3 to 3
- kv_weight: bfloat16 [768, 128], P(('dp', 'seq')), may hold values from -0.21875 to 0.21875
- value_bias: bfloat16 [64], replicated, may hold values from -0.29882812 to 0.29882812
- out_weight: bfloat16 [768, 768], P(('dp', 'seq')), may hold values from -2.5 to 2.5
- out_bias: bfloat16 [768], P(('dp', 'seq')), may hold values from -2 to 2
- norm2_gain: bfloat16 [768], P(('dp', 'seq')), may hold values from 0.099609375 to 1.8984375
- norm2_shift: bfloat16 [768], P(('dp', 'seq')), may hold values from -3 to 3
- fc_weight: bfloat16 [768, 3072], P(('dp', 'seq')), may hold values from -0.21875 to 0.21875
- fc_bias: bfloat16 [3072], P(('dp', 'seq')), may hold values from -3 to 3
- proj_weight: bfloat16 [3072, 768], P(('dp', 'seq')), may hold values from -0.109375 to 0.109375
- proj_bias: bfloat16 [768], P(('dp', 'seq')), may hold values from -2 to 2
Outputs:
- block_out: bfloat16 [2, 8, 1024, 768], P(None, 'dp', 'seq')
- input_grad: float32 [2, 8, 1024, 768], P(None, 'dp', 'seq')
- norm1_gain_grad: float32 [768], P(('dp', 'seq'))
- norm1_shift_grad: float32 [768], P(('dp', 'seq'))
- query_weight_grad: float32 [768, 768], P(('dp', 'seq'))
- query_bias_grad: float32 [768], P(('dp', 'seq'))
- kv_weight_grad: float32 [768, 128], P(('dp', 'seq'))
- value_bias_grad: float32 [64], replicated
- out_weight_grad: float32 [768, 768], P(('dp', 'seq'))
- out_bias_grad: float32 [768], P(('dp', 'seq'))
- norm2_gain_grad: float32 [768], P(('dp', 'seq'))
- norm2_shift_grad: float32 [768], P(('dp', 'seq'))
- fc_weight_grad: float32 [768, 3072], P(('dp', 'seq'))
- fc_bias_grad: float32 [3072], P(('dp', 'seq'))
- proj_weight_grad: float32 [3072, 768], P(('dp', 'seq'))
- proj_bias_grad: float32 [768], P(('dp', 'seq'))
The draws below stay inside these ranges and needn't reach their ends.
Inputs may be any that keep to these rules, and one draw needn't show every extreme that they name: `doc_starts`: each packed sequence's offsets begin with 0 and rise strictly.
All inputs are finite; a program needn't handle non-finite values.
Results may differ from the reference program's by a relative error of at most 0.013.
Values may be sent and summed in bfloat16 or wider, within the bound.
No kernel may reach another device: no remote copies, remote signals or barrier semaphores. Data moves between devices by JAX's collectives and lax.ppermute only.
A program may use at most 192 MiB of HBM per device.

```python
import jax
import jax.numpy as jnp
from jax import lax

D = 768
H = 12
HD = 64
FF = 3072
DOCS = 4
MICRO = 2
LENGTH = 1024
BATCH = 8


def draw_doc_starts(key, part):
    sequence_count = MICRO * BATCH
    subkeys = jax.random.split(key, sequence_count)

    def one_row(subkey):
        shuffled = jax.random.permutation(subkey, LENGTH - 1) + 1
        picked = jnp.sort(shuffled[:DOCS - 1]).astype(jnp.int32)
        return jnp.concatenate([jnp.zeros((1,), jnp.int32), picked])
    table = jax.vmap(one_row)(subkeys)
    table = table.at[0, DOCS - 1].set(LENGTH - 1)
    return table.reshape(MICRO, BATCH, DOCS).astype(jnp.int32)


def block_scale(own_key, dims, pieces, low, top_value):
    level, own = 1.0, jax.random.fold_in(own_key, 6)
    for axis_at, parts in pieces:
        draws = jnp.exp(jax.random.uniform(jax.random.fold_in(own, axis_at), (parts,), jnp.float32, low / len(pieces), top_value / len(pieces)))
        level = level * jnp.repeat(draws, dims[axis_at] // parts).reshape([-1 if axis == axis_at else 1 for axis in range(len(dims))])
    return level


def bell_draw(key, extent, scale, most, cuts=(), kind=jnp.bfloat16):
    gain = block_scale(key, extent, cuts, -0.22, 0.18) if cuts else 1.0
    array = jax.random.normal(key, extent, jnp.float32) * scale * gain
    return jnp.minimum(jnp.maximum(array, -most), most).astype(kind)


def setup_inputs(seed: int = 0) -> dict:
    splits = jax.random.split(jax.random.key(seed), 18)
    tokens = bell_draw(splits[0], (MICRO, BATCH, LENGTH, D), 1.0, 6.0, ((1, 4), (2, 8)))
    doc_starts = draw_doc_starts(jax.random.fold_in(splits[17], 71), 0)
    cotangent = bell_draw(splits[2], (MICRO, BATCH, LENGTH, D), 1.0, 6.0, ((1, 4), (2, 8)))
    norm1_gain = jnp.clip(1.0 + 0.18 * jax.random.normal(splits[3], (D,), jnp.float32), 0.099609375, 1.8984375).astype(jnp.bfloat16)
    norm1_shift = bell_draw(splits[4], (D,), 0.5, 3.0, ((0, 32),))
    query_weight = bell_draw(splits[5], (D, D), D ** -0.5, 0.21875, ((0, 32),))
    query_bias = bell_draw(splits[6], (D,), 0.5, 3.0, ((0, 32),))
    kv_weight = bell_draw(splits[7], (D, 2 * HD), D ** -0.5, 0.21875, ((0, 32),))
    value_bias = bell_draw(splits[8], (HD,), 0.05, 0.29882812)
    out_weight = bell_draw(splits[9], (D, D), (max(D * 2 * DOCS // LENGTH, 1)) ** -0.5, 2.5, ((0, 32),))
    out_bias = bell_draw(splits[10], (D,), 0.3, 2.0, ((0, 32),))
    norm2_gain = jnp.clip(1.0 + 0.18 * jax.random.normal(splits[11], (D,), jnp.float32), 0.099609375, 1.8984375).astype(jnp.bfloat16)
    norm2_shift = bell_draw(splits[12], (D,), 0.5, 3.0, ((0, 32),))
    fc_weight = bell_draw(splits[13], (D, FF), D ** -0.5, 0.21875, ((0, 32),))
    fc_bias = bell_draw(splits[14], (FF,), 0.5, 3.0, ((0, 32),))
    proj_weight = bell_draw(splits[15], (FF, D), FF ** -0.5, 0.109375, ((0, 32),))
    proj_bias = bell_draw(splits[16], (D,), 0.3, 2.0, ((0, 32),))
    return dict(tokens=tokens, doc_starts=doc_starts, cotangent=cotangent, norm1_gain=norm1_gain, norm1_shift=norm1_shift, query_weight=query_weight, query_bias=query_bias, kv_weight=kv_weight, value_bias=value_bias, out_weight=out_weight, out_bias=out_bias, norm2_gain=norm2_gain, norm2_shift=norm2_shift, fc_weight=fc_weight, fc_bias=fc_bias, proj_weight=proj_weight, proj_bias=proj_bias)


HIGHEST_PRECISION = lax.Precision.HIGHEST
EPSILON = 1e-05

@jax.custom_vjp
def low(v):
    return lax.optimization_barrier(v.astype(jnp.bfloat16)).astype(jnp.float32)

@jax.custom_vjp
def low_back(v):
    return v

def low_keep(v):
    return (low(v), None)

def low_pass(kept, grad):
    return (grad,)

def back_keep(v):
    return (v, None)

def back_low(kept, grad):
    return (low(grad),)
low.defvjp(low_keep, low_pass)
low_back.defvjp(back_keep, back_low)

def matmul(left_side, right_side):
    return jnp.dot(left_side, right_side, precision=HIGHEST_PRECISION, preferred_element_type=jnp.float32)

def layer_norm(hidden, gain_row, shift_row):
    centred = hidden - lax.optimization_barrier(jnp.mean(hidden, axis=-1, keepdims=True))
    spread = lax.optimization_barrier(jnp.mean(centred * centred, axis=-1, keepdims=True))
    return centred * lax.rsqrt(spread + EPSILON) * gain_row + shift_row

def forward(hidden, starts, norm1_gain, norm1_shift, query_weight, query_bias, kv_weight, value_bias, out_weight, out_bias, norm2_gain, norm2_shift, fc_weight, fc_bias, proj_weight, proj_bias):
    score_scale = HD ** (-0.5)
    normed = low(layer_norm(hidden, norm1_gain, norm1_shift))
    queries = low(low_back((matmul(normed, query_weight) + query_bias) * score_scale))
    kv_bias = jnp.concatenate([jnp.zeros((HD,), jnp.float32), value_bias])
    kv_both = low(low_back(matmul(normed, kv_weight) + kv_bias))
    key_rows = kv_both[:, :HD]
    value_rows = kv_both[:, HD:]
    positions = jnp.arange(LENGTH, dtype=jnp.int32)
    doc_index = lax.optimization_barrier(jnp.sum((positions[:, None] >= starts[None, :]).astype(jnp.int32), axis=1))
    block_rows = min(256, LENGTH)
    block_starts = jnp.arange(0, LENGTH, block_rows, dtype=jnp.int32)

    def attend(packed):
        query_block, block_first = packed
        rows_here = block_first + jnp.arange(block_rows, dtype=jnp.int32)
        docs_here = lax.dynamic_slice_in_dim(doc_index, block_first, block_rows)
        visible = (positions[None, :] <= rows_here[:, None]) & (doc_index[None, :] == docs_here[:, None])
        scores = low_back(jnp.einsum('bhd,kd->bhk', query_block, key_rows, precision=HIGHEST_PRECISION))
        scores = jnp.where(visible[:, None, :], scores, -1e+30)
        row_top = lax.optimization_barrier(jnp.max(scores, axis=-1, keepdims=True))
        weights = jnp.exp(scores - row_top)
        weights = weights / lax.optimization_barrier(jnp.sum(weights, axis=-1, keepdims=True))
        return jnp.einsum('bhk,kd->bhd', low(weights), value_rows, precision=HIGHEST_PRECISION)
    heads_out = lax.map(jax.checkpoint(attend), (queries.reshape(LENGTH // block_rows, block_rows, H, HD), block_starts))
    mixed_heads = low(low_back(heads_out.reshape(LENGTH, D)))
    branch = low_back(matmul(mixed_heads, out_weight) + out_bias)
    hidden2 = hidden + branch
    normed2 = low(layer_norm(hidden2, norm2_gain, norm2_shift))
    upward = low_back(matmul(normed2, fc_weight) + fc_bias)
    active = low(jax.nn.gelu(upward, approximate=True))
    feed_out = low_back(matmul(active, proj_weight) + proj_bias)
    return hidden2 + feed_out

def reference(tokens, doc_starts, cotangent, norm1_gain, norm1_shift, query_weight, query_bias, kv_weight, value_bias, out_weight, out_bias, norm2_gain, norm2_shift, fc_weight, fc_bias, proj_weight, proj_bias):
    weight_args = tuple((weight_arg.astype(jnp.float32) for weight_arg in (norm1_gain, norm1_shift, query_weight, query_bias, kv_weight, value_bias, out_weight, out_bias, norm2_gain, norm2_shift, fc_weight, fc_bias, proj_weight, proj_bias)))
    flat_tokens = tokens.reshape(MICRO * BATCH, LENGTH, D)
    flat_starts = doc_starts.reshape(MICRO * BATCH, DOCS)
    flat_cotangent = cotangent.reshape(MICRO * BATCH, LENGTH, D)

    def one_sequence(totals, packed):
        hidden, starts, upstream = packed

        def closed(hidden_in, *params):
            return forward(hidden_in, starts, *params)
        result, pullback = jax.vjp(closed, hidden.astype(jnp.float32), *weight_args)
        gradients = pullback(upstream.astype(jnp.float32))
        totals = tuple((earlier + addend for earlier, addend in zip(totals, gradients[1:])))
        return (totals, (result.astype(jnp.bfloat16), gradients[0]))
    zero_grads = tuple((jnp.zeros(weight_arg.shape, jnp.float32) for weight_arg in weight_args))
    totals, (block_out, input_grad) = lax.scan(one_sequence, zero_grads, (flat_tokens, flat_starts, flat_cotangent))
    return (block_out.reshape(tokens.shape), input_grad.reshape(tokens.shape)) + totals
```

```python
import functools

import jax
import jax.numpy as jnp
import numpy as np
from jax import lax
from jax.experimental import pallas as pl
from jax.experimental.pallas import tpu as pltpu
from jax.sharding import PartitionSpec as P

H = 12
HD = 64
EPSILON = 1e-05
AXES = ("dp", "seq")
F32 = jnp.float32
BF16 = jnp.bfloat16
MASKED = -1e30
VMEM_BYTES = 60 * 1024 * 1024


class Plan:
    def __init__(self, dp_size, seq_size):
        self.dp, self.seq, self.count = dp_size, seq_size, dp_size * seq_size
        seq_bits = seq_size.bit_length() - 1
        low = 1
        mid = [1 << bit for bit in range(1, seq_bits)]
        high = [seq_size << bit for bit in range(1, dp_size.bit_length() - 1)]
        self.core = seq_size
        self.weight_orders = [mid[::-1] + [low] + high, high + mid[::-1] + [low]]
        self.kv_orders = [mid[::-1] + [low], [low] + mid[::-1]]
        self.all_order = [low] + mid + high + [self.core]

    def core_of(self, device):
        return (device // self.core) & 1

    def pairs(self, orders, round_index):
        return [(n, n ^ orders[self.core_of(n)][round_index]) for n in range(self.count)]

    def swap(self, values, orders, round_index):
        return lax.ppermute(values, AXES, self.pairs(orders, round_index))

    def swap_core(self, values):
        return lax.ppermute(values, AXES, [(n, n ^ self.core) for n in range(self.count)])

    def offsets(self, orders):
        table = []
        for order in orders:
            slots = [0]
            for mask in order:
                slots = slots + [slot ^ mask for slot in slots]
            table.append(slots)
        return np.asarray(table, np.int32)


def layer_stats(values):
    mean = jnp.mean(values, axis=-1, keepdims=True)
    centred = values - mean
    spread = jnp.mean(centred * centred, axis=-1, keepdims=True)
    return centred, lax.rsqrt(spread + EPSILON)


def layer_back(d_out, unit, inverse, gain):
    scaled = d_out * gain
    first = jnp.mean(scaled, axis=-1, keepdims=True)
    second = jnp.mean(scaled * unit, axis=-1, keepdims=True)
    return inverse * (scaled - first - unit * second)


def tanh_gelu(values):
    return jax.nn.gelu(values, approximate=True)


def product(left_side, right_side):
    return jnp.dot(left_side, right_side, preferred_element_type=F32)


def back_product(left_side, right_side):
    return lax.dot_general(
        left_side, right_side, (((1,), (1,)), ((), ())), preferred_element_type=F32
    )


def outer_sum(left_side, right_side):
    return lax.dot_general(
        left_side, right_side, (((0,), (0,)), ((), ())), preferred_element_type=F32
    )


def column_sums(values):
    return jnp.sum(values.astype(F32), axis=0)


def grouped(rows):
    count = rows.shape[0]
    unit = 8 if count % 8 == 0 else count
    return rows.reshape(count // unit, unit, rows.shape[1])


def gather_rounds(plan, shard):
    orders = plan.weight_orders
    last = len(orders[0]) - 1
    held = shard
    for round_index in range(last):
        held = jnp.concatenate([held, plan.swap(held, orders, round_index)], axis=0)
    other = plan.swap(held, orders, last)
    return held, other, plan.swap_core(held), plan.swap_core(other)


def assemble_kernel(groups, slots, place_ref, first, second, third, fourth, out_ref, sems):
    copies = []
    for part, ref in enumerate((first, second, third, fourth)):
        for slot in range(slots):
            target = place_ref[part * slots + slot]
            copy = pltpu.make_async_copy(
                ref.at[pl.ds(slot * groups, groups)],
                out_ref.at[pl.ds(target * groups, groups)],
                sems.at[part * slots + slot],
            )
            copy.start()
            copies.append(copy)
    for copy in copies:
        copy.wait()


def assemble(plan, parts, place):
    slots = plan.count // 4
    total, unit, width = parts[0].shape
    groups = total // slots
    if unit % 8:
        whole = jnp.concatenate(parts, axis=0).reshape(plan.count, groups * unit, width)
        inverse = jnp.zeros((plan.count,), jnp.int32).at[place].set(
            jnp.arange(plan.count, dtype=jnp.int32)
        )
        return jnp.take(whole, inverse, axis=0).reshape(plan.count * groups * unit, width)
    out = pl.pallas_call(
        functools.partial(assemble_kernel, groups, slots),
        out_shape=jax.ShapeDtypeStruct((4 * total, unit, width), parts[0].dtype),
        grid_spec=pltpu.PrefetchScalarGridSpec(
            num_scalar_prefetch=1,
            grid=(1,),
            in_specs=[pl.BlockSpec(memory_space=pl.ANY)] * 4,
            out_specs=pl.BlockSpec((4 * total, unit, width), lambda i, place: (0, 0, 0)),
            scratch_shapes=[pltpu.SemaphoreType.DMA((plan.count,))],
        ),
        compiler_params=pltpu.CompilerParams(vmem_limit_bytes=VMEM_BYTES),
        name="assemble",
    )(place, *parts)
    return out.reshape(4 * total * unit, width)


def scatter_rounds(plan, sums):
    orders = plan.weight_orders
    for round_index in reversed(range(len(orders[0]))):
        half = sums.shape[0] // 2
        coming = plan.swap(sums[half:].astype(BF16), orders, round_index)
        sums = sums[:half] + coming.astype(F32)
    return sums


def outer_kernel(block_rows, slot_ref, left_ref, left2_ref, right_ref, right2_ref, out_ref, turned):
    tokens = left_ref.shape[0]

    @pl.when(pl.program_id(0) == 0)
    def _():
        turned[:, :tokens] = left_ref[...].T
        turned[:, tokens:] = left2_ref[...].T

    total = jnp.dot(turned[:, :tokens], right_ref[...], preferred_element_type=F32)
    total = total + jnp.dot(turned[:, tokens:], right2_ref[...], preferred_element_type=F32)
    groups = block_rows // 8
    for block in range(total.shape[0] // block_rows):
        piece = total[block * block_rows : (block + 1) * block_rows]
        piece = piece.reshape(groups, 8, piece.shape[1])
        out_ref[pl.ds(slot_ref[block] * groups, groups)] = piece


def outer_slots(plan, left, left2, right, right2, slot_of):
    tokens, rows = left.shape
    width = right.shape[1]
    blocks = plan.count // 2
    block_rows = rows // blocks
    if block_rows % 8:
        sums = outer_sum(left, right) + outer_sum(left2, right2)
        inverse = jnp.zeros((blocks,), jnp.int32).at[slot_of].set(jnp.arange(blocks, dtype=jnp.int32))
        return jnp.take(sums.reshape(blocks, block_rows, width), inverse, axis=0)
    tile = width
    while rows * tile > 768 * 512 and tile % 256 == 0:
        tile //= 2
    return pl.pallas_call(
        functools.partial(outer_kernel, block_rows),
        out_shape=jax.ShapeDtypeStruct((rows // 8, 8, width), F32),
        grid_spec=pltpu.PrefetchScalarGridSpec(
            num_scalar_prefetch=1,
            grid=(width // tile,),
            in_specs=[
                pl.BlockSpec((tokens, rows), lambda i, slot: (0, 0)),
                pl.BlockSpec((tokens, rows), lambda i, slot: (0, 0)),
                pl.BlockSpec((tokens, tile), lambda i, slot: (0, i)),
                pl.BlockSpec((tokens, tile), lambda i, slot: (0, i)),
            ],
            out_specs=pl.BlockSpec((rows // 8, 8, tile), lambda i, slot: (0, 0, i)),
            scratch_shapes=[pltpu.VMEM((rows, 2 * tokens), BF16)],
        ),
        compiler_params=pltpu.CompilerParams(vmem_limit_bytes=VMEM_BYTES),
        name="outer",
    )(slot_of, left, left2, right, right2)


def stack_heads(rows_ref_value):
    turned = rows_ref_value.astype(F32).T
    return jnp.concatenate([turned[h * HD : (h + 1) * HD] for h in range(H)], axis=1)


def unstack_heads(stacked, rows):
    turned = jnp.concatenate([stacked[:, h * rows : (h + 1) * rows] for h in range(H)], axis=0)
    return turned.T


def in_document(positions, starts_ref, sequence, doc, docs):
    inside = positions >= starts_ref[sequence, doc]
    if doc + 1 < docs:
        inside = inside & (positions < starts_ref[sequence, doc + 1])
    return inside


def query_operand(stacked, positions, starts_ref, sequence, docs):
    lower = jnp.zeros((HD, stacked.shape[1]), F32)
    row = lax.broadcasted_iota(jnp.int32, lower.shape, 0)
    for doc in range(docs):
        outside = jnp.where(in_document(positions, starts_ref, sequence, doc, docs), 0.0, 1.0)
        lower = jnp.where(row == doc, outside, lower)
    return jnp.concatenate([stacked, lower], axis=0).astype(BF16)


def key_operand(pair, positions, starts_ref, sequence, docs):
    lane = lax.broadcasted_iota(jnp.int32, pair.shape, 1)
    extra = jnp.zeros(pair.shape, F32)
    for doc in range(docs):
        inside = in_document(positions, starts_ref, sequence, doc, docs)
        extra = jnp.where((lane == HD + doc) & inside, MASKED, extra)
    return jnp.where(lane < HD, pair.astype(F32), extra).astype(BF16)


def pair_bounds(meta_ref, starts_ref, sequence, rows, docs):
    mine = meta_ref[0]
    first_row = mine * rows
    first_key = jnp.int32(0)
    for doc in range(docs):
        start = starts_ref[sequence, doc]
        first_key = jnp.where(start <= first_row, start, first_key)
    return first_key // (2 * rows), mine // 2, first_row


def load_pair(meta_ref, kv_ref, pair, rows):
    keys = jnp.concatenate(
        [kv_ref[meta_ref[1 + 2 * pair], 0], kv_ref[meta_ref[2 + 2 * pair], 0]], axis=0
    )
    positions = pair * 2 * rows + lax.broadcasted_iota(jnp.int32, keys.shape, 0)
    return keys, positions


def dot_nn(left, right):
    return jnp.dot(left, right, preferred_element_type=F32)


def dot_nt(left, right):
    return lax.dot_general(left, right, (((1,), (1,)), ((), ())), preferred_element_type=F32)


def query_positions(first_row, rows):
    lane = lax.broadcasted_iota(jnp.int32, (1, H * rows), 1)
    return first_row + lax.rem(lane, rows)


def attend_kernel(rows, docs, meta_ref, starts_ref, q_ref, kv_ref, mixed_ref, out_ref, lse_ref,
                  query_s, top_s, total_s, sum_s):
    sequence = pl.program_id(0)
    low, high, first_row = pair_bounds(meta_ref, starts_ref, sequence, rows, docs)
    positions = query_positions(first_row, rows)
    query_s[...] = query_operand(stack_heads(q_ref[0]), positions, starts_ref, sequence, docs)

    def visit(pair, first):
        keys, key_at = load_pair(meta_ref, kv_ref, pair, rows)
        scores = dot_nn(key_operand(keys, key_at, starts_ref, sequence, docs), query_s[...])
        if first:
            scores = jnp.where(key_at[:, :1] <= positions, scores, MASKED)
        top = jnp.max(scores, axis=0, keepdims=True)
        if not first:
            top = jnp.maximum(top, top_s[...])
        weights = jnp.exp(scores - top)
        total = jnp.sum(weights, axis=0, keepdims=True)
        turned = keys.astype(F32).T.astype(BF16)
        part = dot_nn(turned, weights.astype(BF16))
        if not first:
            fade = jnp.exp(top_s[...] - top)
            total = total + total_s[...] * fade
            part = part + sum_s[...] * fade
        top_s[...] = top
        total_s[...] = total
        sum_s[...] = part

    visit(high, True)

    @pl.loop(low, high)
    def _(pair):
        visit(pair, False)

    out = sum_s[HD:, :] / total_s[...]
    out_ref[0] = out
    mixed_ref[0] = unstack_heads(out, rows).astype(BF16)
    lse_ref[0] = top_s[...] + jnp.log(total_s[...])


def attend_back_kernel(rows, docs, meta_ref, starts_ref, q_ref, kv_ref, d_ref, out_ref, lse_ref,
                       dq_ref, dkv_ref, vsum_ref, query_s, plain_s, grad_s, delta_s, dq_s):
    sequence = pl.program_id(0)
    low, high, first_row = pair_bounds(meta_ref, starts_ref, sequence, rows, docs)
    positions = query_positions(first_row, rows)
    stacked = stack_heads(q_ref[0])
    query_s[...] = query_operand(stacked, positions, starts_ref, sequence, docs)
    nothing = jnp.zeros(stacked.shape, F32)
    plain_s[...] = jnp.concatenate([stacked, nothing], axis=0).astype(BF16)
    grads = stack_heads(d_ref[0])
    grad_s[...] = jnp.concatenate([nothing, grads], axis=0).astype(BF16)
    delta_s[...] = jnp.sum(grads * out_ref[0], axis=0, keepdims=True)
    dkv_ref[...] = jnp.zeros(dkv_ref.shape, dkv_ref.dtype)
    vsum_ref[...] = jnp.zeros(vsum_ref.shape, vsum_ref.dtype)

    def visit(pair, first):
        keys, key_at = load_pair(meta_ref, kv_ref, pair, rows)
        scores = dot_nn(key_operand(keys, key_at, starts_ref, sequence, docs), query_s[...])
        probs = jnp.exp(scores - lse_ref[0])
        if first:
            probs = jnp.where(key_at[:, :1] <= positions, probs, 0.0)
        d_probs = dot_nn(keys, grad_s[...])
        d_scores = (probs * (d_probs - delta_s[...])).astype(BF16)
        d_keys = dot_nt(d_scores, plain_s[...]) + dot_nt(probs.astype(BF16), grad_s[...])
        vsum_ref[0] += jnp.sum(d_keys, axis=0, keepdims=True)
        low_keys = d_keys.astype(BF16)
        dkv_ref[meta_ref[1 + 2 * pair], 0] = low_keys[:rows]
        dkv_ref[meta_ref[2 + 2 * pair], 0] = low_keys[rows:]
        turned = keys.astype(F32).T.astype(BF16)
        part = dot_nn(turned, d_scores)
        dq_s[...] = part if first else dq_s[...] + part

    visit(high, True)

    @pl.loop(low, high)
    def _(pair):
        visit(pair, False)

    dq_ref[0] = unstack_heads(dq_s[:HD, :], rows).astype(BF16)


def attention_specs(slots, sequences, rows):
    width = H * HD
    per_token = pl.BlockSpec((1, rows, width), lambda i, meta, starts: (i, 0, 0))
    per_key = pl.BlockSpec((slots, 1, rows, 2 * HD), lambda i, meta, starts: (0, i, 0, 0))
    stacked = pl.BlockSpec((1, HD, H * rows), lambda i, meta, starts: (i, 0, 0))
    line = pl.BlockSpec((1, 1, H * rows), lambda i, meta, starts: (i, 0, 0))
    short = pl.BlockSpec((1, 1, 2 * HD), lambda i, meta, starts: (i, 0, 0))
    return per_token, per_key, stacked, line, short


def attend(meta, starts, queries, kv_slots):
    sequences, rows, width = queries.shape
    slots = kv_slots.shape[0]
    per_token, per_key, stacked, line, _ = attention_specs(slots, sequences, rows)
    lanes = H * rows
    return pl.pallas_call(
        functools.partial(attend_kernel, rows, starts.shape[1]),
        out_shape=(
            jax.ShapeDtypeStruct((sequences, rows, width), BF16),
            jax.ShapeDtypeStruct((sequences, HD, lanes), F32),
            jax.ShapeDtypeStruct((sequences, 1, lanes), F32),
        ),
        grid_spec=pltpu.PrefetchScalarGridSpec(
            num_scalar_prefetch=2,
            grid=(sequences,),
            in_specs=[per_token, per_key],
            out_specs=(per_token, stacked, line),
            scratch_shapes=[
                pltpu.VMEM((2 * HD, lanes), BF16),
                pltpu.VMEM((1, lanes), F32),
                pltpu.VMEM((1, lanes), F32),
                pltpu.VMEM((2 * HD, lanes), F32),
            ],
        ),
        compiler_params=pltpu.CompilerParams(vmem_limit_bytes=VMEM_BYTES),
        name="attend",
    )(meta, starts, queries, kv_slots)


def attend_back(meta, starts, queries, kv_slots, d_mixed, out, lse):
    sequences, rows, width = queries.shape
    slots = kv_slots.shape[0]
    per_token, per_key, stacked, line, short = attention_specs(slots, sequences, rows)
    lanes = H * rows
    return pl.pallas_call(
        functools.partial(attend_back_kernel, rows, starts.shape[1]),
        out_shape=(
            jax.ShapeDtypeStruct((sequences, rows, width), BF16),
            jax.ShapeDtypeStruct(kv_slots.shape, BF16),
            jax.ShapeDtypeStruct((sequences, 1, 2 * HD), F32),
        ),
        grid_spec=pltpu.PrefetchScalarGridSpec(
            num_scalar_prefetch=2,
            grid=(sequences,),
            in_specs=[per_token, per_key, per_token, stacked, line],
            out_specs=(per_token, per_key, short),
            scratch_shapes=[
                pltpu.VMEM((2 * HD, lanes), BF16),
                pltpu.VMEM((2 * HD, lanes), BF16),
                pltpu.VMEM((2 * HD, lanes), BF16),
                pltpu.VMEM((1, lanes), F32),
                pltpu.VMEM((2 * HD, lanes), F32),
            ],
        ),
        compiler_params=pltpu.CompilerParams(vmem_limit_bytes=VMEM_BYTES),
        name="attend_back",
    )(meta, starts, queries, kv_slots, d_mixed, out, lse)


def body(plan, tokens, doc_starts, cotangent, norm1_gain, norm1_shift, query_weight, query_bias,
         kv_weight, value_bias, out_weight, out_bias, norm2_gain, norm2_shift, fc_weight, fc_bias,
         proj_weight, proj_bias):
    micro_count, seq_count, row_count, width = tokens.shape
    sequences = micro_count * seq_count
    token_count = sequences * row_count
    shard_rows = query_weight.shape[0]
    hidden_units = fc_weight.shape[1]
    ratio = hidden_units // width
    slots = plan.count // 2
    score_scale = HD ** (-0.5)
    small_width = 128

    seq_index = lax.axis_index("seq")
    device = lax.axis_index("dp") * plan.seq + seq_index
    core = (device // plan.core) & 1

    weight_offsets = plan.offsets(plan.weight_orders)
    mine = jnp.asarray(weight_offsets)[core] ^ device
    other = jnp.asarray(weight_offsets)[1 - core] ^ device ^ plan.core
    place = jnp.concatenate([mine, other]).astype(jnp.int32)
    kind = np.arange(plan.count).reshape(-1, 2, plan.core).transpose(1, 0, 2).reshape(2, -1)
    kind_of = jnp.asarray(kind.astype(np.int32))[core]
    slot_of = jnp.argmax((kind_of[:, None] == mine[None, :]).astype(jnp.int32), axis=1)
    slot_of = slot_of.astype(jnp.int32)
    kv_seq = (jnp.asarray(plan.offsets(plan.kv_orders))[core] ^ seq_index).astype(jnp.int32)
    natural = jnp.arange(plan.seq, dtype=jnp.int32)
    kv_slot_of = jnp.argmax((natural[:, None] == kv_seq[None, :]).astype(jnp.int32), axis=1)
    meta = jnp.concatenate([seq_index[None].astype(jnp.int32), kv_slot_of.astype(jnp.int32)])
    starts = doc_starts.reshape(sequences, doc_starts.shape[2])

    small = jnp.stack(
        [norm1_gain, norm1_shift, query_bias, out_bias, norm2_gain, norm2_shift, proj_bias], axis=1
    )
    small = jnp.concatenate([small, fc_bias.reshape(shard_rows, ratio)], axis=1)
    small = jnp.pad(small, ((0, 0), (0, small_width - small.shape[1])))
    first_shard = jnp.concatenate([query_weight, kv_weight, small, out_weight], axis=1)
    qkv_width = width + 2 * HD
    w_first = assemble(plan, gather_rounds(plan, grouped(first_shard)), place)
    w_fc = assemble(plan, gather_rounds(plan, grouped(fc_weight)), place)
    w_proj = assemble(plan, gather_rounds(plan, grouped(proj_weight)), place)
    w_qkv = w_first[:, :qkv_width]
    w_out = w_first[:, qkv_width + small_width :]
    small_full = w_first[:, qkv_width : qkv_width + small_width].astype(F32)
    rows_full = small_full[:, :7].T
    gain_one, shift_one, b_query, b_out, gain_two, shift_two, b_proj = [rows_full[i] for i in range(7)]
    b_fc = small_full[:, 7 : 7 + ratio].reshape(hidden_units)

    hidden = tokens.reshape(token_count, width).astype(F32)
    grad_out = cotangent.reshape(token_count, width)
    centred, inverse_one = layer_stats(hidden)
    normed = (centred * inverse_one * gain_one + shift_one).astype(BF16)
    qkv_bias = jnp.concatenate([b_query, jnp.zeros((HD,), F32), value_bias.astype(F32)])
    qkv_scale = jnp.concatenate([jnp.full((width,), score_scale, F32), jnp.ones((2 * HD,), F32)])
    qkv = ((product(normed, w_qkv) + qkv_bias) * qkv_scale).astype(BF16)
    queries = qkv[:, :width].reshape(sequences, row_count, width)
    kv_slots = qkv[:, width:].reshape(1, sequences, row_count, 2 * HD)
    for round_index in range(len(plan.kv_orders[0])):
        coming = plan.swap(kv_slots, plan.kv_orders, round_index)
        kv_slots = jnp.concatenate([kv_slots, coming], axis=0)
    mixed, attended, lse = attend(meta, starts, queries, kv_slots)
    mixed = mixed.reshape(token_count, width)
    hidden2 = hidden + (product(mixed, w_out) + b_out)
    centred2, inverse_two = layer_stats(hidden2)
    unit_two = centred2 * inverse_two
    normed2 = (unit_two * gain_two + shift_two).astype(BF16)
    upward = product(normed2, w_fc) + b_fc
    active = tanh_gelu(upward).astype(BF16)
    result = hidden2 + (product(active, w_proj) + b_proj)
    block_out = result.astype(BF16).reshape(tokens.shape)

    def halves(values):
        view = values.reshape(token_count, -1, 2, values.shape[1] * plan.core // plan.count)
        zero, one = view[:, :, 0], view[:, :, 1]
        keep = jnp.where(core == 0, zero, one).reshape(token_count, -1)
        send = jnp.where(core == 0, one, zero).reshape(token_count, -1)
        return keep, plan.swap_core(send)

    grad_out2 = plan.swap_core(grad_out)
    active_half, active_half2 = halves(active)
    proj_sums = outer_slots(plan, active_half, active_half2, grad_out, grad_out2, slot_of)
    proj_grad = scatter_rounds(plan, proj_sums)

    d_active = back_product(grad_out, w_proj)
    gelu_value, gelu_back = jax.vjp(tanh_gelu, upward)
    d_upward = gelu_back(d_active)[0].astype(BF16)
    d_upward2 = plan.swap_core(d_upward)
    normed2_half, normed2_half2 = halves(normed2)
    fc_sums = outer_slots(plan, normed2_half, normed2_half2, d_upward, d_upward2, slot_of)
    fc_grad = scatter_rounds(plan, fc_sums)
    d_normed2 = back_product(d_upward, w_fc)
    d_hidden2 = grad_out.astype(F32) + layer_back(d_normed2, unit_two, inverse_two, gain_two)
    d_branch = d_hidden2.astype(BF16)

    d_mixed = back_product(d_branch, w_out).astype(BF16).reshape(sequences, row_count, width)
    d_queries, d_kv_slots, value_sums = attend_back(
        meta, starts, queries, kv_slots, d_mixed, attended, lse
    )
    d_queries = d_queries.reshape(token_count, width)
    for round_index in reversed(range(len(plan.kv_orders[0]))):
        half = d_kv_slots.shape[0] // 2
        coming = plan.swap(d_kv_slots[half:].astype(BF16), plan.kv_orders, round_index)
        d_kv_slots = d_kv_slots[:half].astype(F32) + coming.astype(F32)
    d_kv = d_kv_slots.astype(BF16).reshape(token_count, 2 * HD)
    d_qkv = jnp.concatenate([d_queries, d_kv], axis=1)
    d_branch2 = plan.swap_core(d_branch)
    mixed_half, mixed_half2 = halves(mixed)
    out_sums = outer_slots(plan, mixed_half, mixed_half2, d_branch, d_branch2, slot_of)
    d_qkv2 = plan.swap_core(d_qkv)
    normed_half, normed_half2 = halves(normed)
    qkv_sums = outer_slots(plan, normed_half, normed_half2, d_qkv, d_qkv2, slot_of)
    d_normed = back_product(d_queries, w_qkv[:, :width]) * score_scale + back_product(
        d_kv, w_qkv[:, width:]
    )
    unit_one = centred * inverse_one
    d_hidden = d_hidden2 + layer_back(d_normed, unit_one, inverse_one, gain_one)
    input_grad = d_hidden.reshape(tokens.shape)

    vectors = [
        jnp.sum(d_normed * unit_one, axis=0),
        jnp.sum(d_normed, axis=0),
        column_sums(d_queries) * score_scale,
        column_sums(d_branch),
        jnp.sum(d_normed2 * unit_two, axis=0),
        jnp.sum(d_normed2, axis=0),
        column_sums(grad_out),
    ]
    packed = jnp.concatenate(
        [jnp.stack(vectors).reshape(7, plan.count, shard_rows).transpose(1, 0, 2).reshape(plan.count, -1),
         column_sums(d_upward).reshape(plan.count, -1)], axis=1
    )
    packed = packed + plan.swap_core(packed)
    packed = jnp.take(packed, mine, axis=0)
    small_count = packed.shape[1]
    block = qkv_sums.reshape(slots, shard_rows, qkv_width)
    packed = jnp.pad(packed, ((0, 0), (0, shard_rows * small_width - small_count)))
    first_sums = jnp.concatenate(
        [block, packed.reshape(slots, shard_rows, small_width),
         out_sums.reshape(slots, shard_rows, width)], axis=2
    )
    first_grad = scatter_rounds(plan, first_sums)[0]
    small_grad = first_grad[:, qkv_width : qkv_width + small_width].reshape(-1)
    gain_one_grad, shift_one_grad, query_bias_grad, out_bias_grad, gain_two_grad, shift_two_grad, proj_bias_grad = [
        small_grad[i * shard_rows : (i + 1) * shard_rows] for i in range(7)
    ]
    fc_bias_grad = small_grad[7 * shard_rows : (7 + ratio) * shard_rows]

    value_total = jnp.sum(value_sums, axis=(0, 1))[HD:].reshape(1, HD)
    for mask in plan.all_order:
        pairs = [(n, n ^ mask) for n in range(plan.count)]
        value_total = value_total + lax.ppermute(value_total, AXES, pairs)

    return (
        block_out,
        input_grad,
        gain_one_grad,
        shift_one_grad,
        first_grad[:, :width] * score_scale,
        query_bias_grad,
        first_grad[:, width:qkv_width],
        value_total.reshape(HD),
        first_grad[:, qkv_width + small_width :],
        out_bias_grad,
        gain_two_grad,
        shift_two_grad,
        fc_grad.reshape(fc_weight.shape),
        fc_bias_grad,
        proj_grad.reshape(proj_weight.shape),
        proj_bias_grad,
    )


def solution(mesh):
    plan = Plan(mesh.shape["dp"], mesh.shape["seq"])
    tokens = P(None, "dp", "seq", None)
    vector = P(("dp", "seq"))
    matrix = P(("dp", "seq"), None)
    return jax.shard_map(
        functools.partial(body, plan),
        mesh=mesh,
        in_specs=(
            tokens, P(None, "dp", None), tokens, vector, vector, matrix, vector, matrix, P(),
            matrix, vector, vector, vector, matrix, vector, matrix, vector,
        ),
        out_specs=(
            tokens, tokens, vector, vector, matrix, vector, matrix, P(), matrix, vector, vector,
            vector, matrix, vector, matrix, vector,
        ),
        check_vma=False,
    )
```
